1024 devices in a mesh: dp: 128 (over x, z, core), tensor: 8 (over y).
Axes of the slice: x: 4, y: 8, z: 16, core: 2. Of those that a mesh axis runs over, the one named last changes fastest.
Arguments:
- hidden: bfloat16 [16384, 28672], P('dp', 'tensor'), may hold values from -6 to 6
- out_grad: bfloat16 [16384, 8192], P('dp'), may hold values from -24 to 24
- prev_hidden: bfloat16 [16384, 28672], P('dp', 'tensor'), may hold values from -6 to 6
- prev_grad: bfloat16 [16384, 8192], P('dp'), may hold values from -24 to 24
- prev_basis: float32 [28672, 32], P('tensor'), may hold values from -6 to 6
- warm_start: float32 [8192, 32], replicated, may hold values from -0.17 to 0.17
Outputs:
- new_basis: float32 [28672, 32], P('tensor')
- new_factor: float32 [8192, 32], P('dp')
The draws below stay inside these ranges and needn't reach their ends.
All inputs are finite; a program needn't handle non-finite values.
Results may differ from the reference program's by a relative error of at most 0.007.
Values sent between devices are 32-bit elements; how exact they have to be, the bound alone decides.
A program may use at most 32 MiB of HBM per device.

```python
import jax
import jax.numpy as jnp
from jax import lax

D = 8192
FF = 28672
R = 32
TOKENS = 16384
N_DP = 128


def strengthened(array, rng, source, target, parts, factor):
    def block_of(dim):
        return (jnp.arange(array.shape[dim]) // (array.shape[dim] // parts)).reshape((-1,) + (1,) * (array.ndim - 1 - dim))

    near = jax.random.permutation(rng, parts)[block_of(target)]
    far = (block_of(target) + parts // 2) % parts
    return jnp.where((block_of(source) == near) | (block_of(source) == far), factor * array, array)


def levels(own_key, extent, shards, smallest, largest):
    factor_of = 1.0
    for dim, shards_of in shards:
        draws = jax.random.uniform(jax.random.fold_in(jax.random.fold_in(own_key, 6), dim), (shards_of,), jnp.float32, smallest / len(shards), largest / len(shards))
        factor_of = factor_of * jnp.repeat(jnp.exp(draws), extent[dim] // shards_of).reshape((-1,) + (1,) * (len(extent) - 1 - dim))
    return factor_of


def bell_draw(key, extent, width, reach, shards=(), held_as=jnp.bfloat16):
    array = width * jax.random.normal(key, extent, jnp.float32)
    if shards:
        array = array * levels(key, extent, shards, -0.22, 0.18)
    return jnp.clip(array, -reach, reach).astype(held_as)


def bell_draw_with(key, shape, scale, limit, split, heavy, held_as=jnp.bfloat16):
    array = scale * jax.random.normal(key, shape, jnp.float32)
    if split:
        array = array * levels(key, shape, split, -0.22, 0.18)
    return jnp.clip(strengthened(array, jax.random.fold_in(key, 3), *heavy), -limit, limit).astype(held_as)


def setup_inputs(seed: int = 0) -> dict:
    keys = jax.random.split(jax.random.key(seed), 7)
    return {
        "hidden": bell_draw(keys[0], (TOKENS, FF), 1.0, 6.0, ((0, 128), (1, 8))),
        "out_grad": bell_draw_with(keys[1], (TOKENS, D), 1.0, 24.0, ((0, 128),), (0, 1, 128, 5.5)),
        "prev_hidden": bell_draw(keys[2], (TOKENS, FF), 1.0, 6.0, ((0, 128), (1, 8))),
        "prev_grad": bell_draw_with(keys[3], (TOKENS, D), 1.0, 24.0, ((0, 128),), (0, 1, 128, 5.5)),
        "prev_basis": bell_draw(keys[4], (FF, R), 1.0, 6.0, ((0, 8),), jnp.float32),
        "warm_start": bell_draw(keys[5], (D, R), 0.028, 0.17, (), jnp.float32),
    }


def reference(hidden, out_grad, prev_hidden, prev_grad, prev_basis, warm_start):
    highest = lax.Precision.HIGHEST
    warm_low = warm_start.astype(jnp.bfloat16)
    projected = jnp.dot(out_grad.astype(jnp.float32), warm_low.astype(jnp.float32), preferred_element_type=jnp.float32).astype(jnp.bfloat16)
    projected_prev = jnp.dot(prev_grad.astype(jnp.float32), warm_low.astype(jnp.float32), preferred_element_type=jnp.float32).astype(jnp.bfloat16)
    coupling = jnp.dot(warm_start.T, warm_start, precision=highest)
    summed = jnp.dot(hidden.T.astype(jnp.float32), projected.astype(jnp.float32), preferred_element_type=jnp.float32) + jnp.dot(prev_hidden.T.astype(jnp.float32), projected_prev.astype(jnp.float32), preferred_element_type=jnp.float32)
    p_mean = summed / N_DP - jnp.dot(prev_basis, coupling, precision=highest)
    gram_matrix = jnp.dot(p_mean.T, p_mean, precision=highest)
    lower = jnp.linalg.cholesky(gram_matrix)
    norm_scale = jnp.sqrt(jnp.float32(FF))
    new_basis = norm_scale * jax.scipy.linalg.solve_triangular(lower, p_mean.T, lower=True).T
    basis_low = new_basis.astype(jnp.bfloat16)
    pulled = jnp.dot(hidden.astype(jnp.float32), basis_low.astype(jnp.float32), preferred_element_type=jnp.float32).astype(jnp.bfloat16)
    pulled_prev = jnp.dot(prev_hidden.astype(jnp.float32), basis_low.astype(jnp.float32), preferred_element_type=jnp.float32).astype(jnp.bfloat16)
    cross_basis = jnp.dot(prev_basis.T, new_basis, precision=highest)
    summed_q = jnp.dot(out_grad.T.astype(jnp.float32), pulled.astype(jnp.float32), preferred_element_type=jnp.float32) + jnp.dot(prev_grad.T.astype(jnp.float32), pulled_prev.astype(jnp.float32), preferred_element_type=jnp.float32)
    new_factor = (summed_q / N_DP - jnp.dot(warm_start, cross_basis, precision=highest)) / norm_scale
    return (new_basis, new_factor)
```

```python
import jax
import jax.numpy as jnp
from jax import lax
from jax.experimental import pallas as pl
from jax.experimental.pallas import tpu as pltpu
from jax.sharding import PartitionSpec as P

MESH = pl.DeviceIdType.MESH
F32, BF16 = jnp.float32, jnp.bfloat16
HIGHEST = lax.Precision.HIGHEST
NT = (((1,), (1,)), ((), ()))
NN = (((1,), (0,)), ((), ()))

NX, NY, NZ, NC = 4, 8, 16, 2
R = 32
FF_ALL, FF, D, TOK = 28672, 3584, 8192, 128
REPLICAS = NX * NZ * NC
HALF = FF // NC
TILES = HALF // 128
G_CHUNKS = 4


def dot(a, b, dims, precision=None):
    return lax.dot_general(a, b, dims, precision=precision, preferred_element_type=F32)


def three_terms(v):
    a = v.astype(BF16).astype(F32)
    r = v - a
    b = r.astype(BF16).astype(F32)
    return a, b, r - b


def inverse_cholesky(gram):
    rows = lax.broadcasted_iota(jnp.int32, (R, 128), 0)
    lanes = lax.broadcasted_iota(jnp.int32, (R, 128), 1)
    m = jnp.where(lanes < R, gram, jnp.where(lanes - R == rows, 1.0, 0.0))
    for k in range(R):
        pivot = m[k : k + 1, k : k + 1]
        inv = lax.rsqrt(pivot)
        inv = inv * (1.5 - 0.5 * pivot * inv * inv)
        row = m[k : k + 1, :] * inv
        column = m[:, k : k + 1] * inv
        m = jnp.where(rows > k, m - column * row, jnp.where(rows == k, row, m))
    return m[:, R : 2 * R]


def kernel(
    hidden, out_grad, prev_hidden, prev_grad, basis_t, warm_t,
    new_basis_t, new_factor_t,
    hid, grad, pb, warm, warm_low,
    s_core, own, r_core, s_x, r_x, s_z, r_z, corr, full, own_tile,
    s_y, r_y, gram_all, s_q, r_qc, s_qx, r_qx, s_qz, r_qz, s_f, r_f, basis_out,
    load_sem, out_sem, send, recv,
):
    dp, y = lax.axis_index("dp"), lax.axis_index("tensor")
    core = lax.rem(dp, NC)
    z = lax.rem(dp // NC, NZ)
    x = dp // (NC * NZ)
    other = 1 - core

    def at(px, pz, pc, py):
        return ((px * NZ + pz) * NC + pc, py)

    partner = at(x, z, other, y)
    x_peers = [at(lax.rem(x + k, NX), z, core, y) for k in range(1, NX)]

    def remote(phase, src, dst, device):
        return pltpu.make_async_remote_copy(
            src_ref=src, dst_ref=dst, send_sem=send.at[phase], recv_sem=recv.at[phase],
            device_id=device, device_id_type=MESH,
        )

    def wait_on(sem, ref):
        pltpu.make_async_copy(ref, ref, sem).wait()

    loads = [pltpu.make_async_copy(warm_t, warm, load_sem.at[0])]
    width = D // G_CHUNKS
    for j in range(G_CHUNKS):
        cols = pl.ds(j * width, width)
        for s, g in enumerate((out_grad, prev_grad)):
            loads.append(
                pltpu.make_async_copy(g.at[:, cols], grad.at[s, :, cols], load_sem.at[1 + 2 * j + s])
            )
    n = 1 + 2 * G_CHUNKS
    loads.append(pltpu.make_async_copy(hidden, hid.at[pl.ds(0, TOK), :], load_sem.at[n]))
    loads.append(pltpu.make_async_copy(prev_hidden, hid.at[pl.ds(TOK, TOK), :], load_sem.at[n + 1]))
    loads.append(pltpu.make_async_copy(basis_t, pb, load_sem.at[n + 2]))
    for copy in loads:
        copy.start()

    barrier = pltpu.get_barrier_semaphore()

    def greet(device):
        pl.semaphore_signal(barrier, inc=1, device_id=device, device_id_type=MESH)

    greet(partner)
    for device in x_peers:
        greet(device)
    for k in range(1, NZ):
        greet(at(x, lax.rem(z + k, NZ), core, y))
    for k in range(1, NY):
        greet(at(x, z, core, lax.rem(y + k, NY)))
        greet(at(x, z, other, lax.rem(y + k, NY)))

    loads[0].wait()
    warm_low[...] = warm[...].astype(BF16)
    acc = [jnp.zeros((R, TOK), F32), jnp.zeros((R, TOK), F32)]
    for j in range(G_CHUNKS):
        cols = slice(j * width, (j + 1) * width)
        for s in range(2):
            loads[1 + 2 * j + s].wait()
            acc[s] = acc[s] + dot(warm_low[:, cols], grad[s, :, cols], NT)
    projected = jnp.concatenate(acc, axis=1).astype(BF16)

    loads[n].wait()
    loads[n + 1].wait()
    my_half = pl.ds(pl.multiple_of(core * HALF, 128), HALF)
    other_half = pl.ds(pl.multiple_of(other * HALF, 128), HALF)
    s_core[...] = dot(projected, hid[:, other_half], NN)
    pl.semaphore_wait(barrier, 1 + (NX - 1) + (NZ - 1) + 2 * (NY - 1))
    remote(0, s_core, r_core, partner).start()
    own[...] = dot(projected, hid[:, my_half], NN)
    wait_on(recv.at[0], r_core)
    s_x[...] = own[...] + r_core[...]

    for k in range(1, NX):
        group = pl.ds(pl.multiple_of(lax.rem(x + k, NX) * 8, 8), 8)
        remote(1, s_x.at[group, :], r_x.at[k - 1], x_peers[k - 1]).start()
    wait_on(recv.at[1], r_x)
    my_rows = pl.ds(pl.multiple_of(x * 8, 8), 8)
    summed = s_x[my_rows, :] + r_x[0] + r_x[1] + r_x[2]
    for j in range(TILES):
        s_z[j] = summed[:, 128 * j : 128 * (j + 1)]

    owner = z < TILES
    for k in range(1, NZ):
        target = lax.rem(z + k, NZ)

        @pl.when(target < TILES)
        def _():
            remote(2, s_z.at[target], r_z.at[k - 1], at(x, target, core, y)).start()

    loads[n + 2].wait()
    tile = jnp.minimum(z, TILES - 1)
    my_tile = pl.ds(pl.multiple_of(core * HALF + tile * 128, 128), 128)
    coupling = dot(warm[...], warm[...], NT, HIGHEST)
    corr[...] = dot(coupling, pb[:, my_tile], NN, HIGHEST)

    @pl.when(owner)
    def _():
        wait_on(recv.at[2], r_z)
        total = s_z[z]
        for k in range(NZ - 1):
            total = total + r_z[k]
        own_tile[...] = total * (1.0 / REPLICAS) - corr[my_rows, :]
        full[my_rows, my_tile] = own_tile[...]
        for k in range(1, NZ):
            target = lax.rem(z + k, NZ)
            remote(3, own_tile, full.at[my_rows, my_tile], at(x, target, core, y)).start()
        wait_on(recv.at[3], full.at[pl.ds(0, 8), pl.ds(0, 128 * (TILES - 1))])

    @pl.when(jnp.logical_not(owner))
    def _():
        wait_on(recv.at[3], full.at[pl.ds(0, 8), pl.ds(0, 128 * TILES)])

    piece = full.at[my_rows, my_half]
    for device in x_peers:
        remote(4, piece, piece, device).start()
    wait_on(recv.at[4], r_x)
    mine = full.at[:, my_half]
    remote(5, mine, mine, partner).start()

    def pulled_half(cols):
        terms = jnp.concatenate(three_terms(full[:, cols]), axis=0).astype(BF16)
        return dot(terms, hid[:, cols], NT)

    zt = pulled_half(my_half)
    wait_on(recv.at[5], r_core)
    zt = zt + pulled_half(other_half)
    zt = zt[0:R] + zt[R : 2 * R] + zt[2 * R : 3 * R]

    for g in range(4):
        for s in range(2):
            s_y[2 * g + s] = zt[8 * g : 8 * (g + 1), 128 * s : 128 * (s + 1)]
    y_peers = [lax.rem(y + k, NY) for k in range(1, NY)]
    for k in range(1, NY):
        target = y_peers[k - 1]
        remote(6, s_y.at[target], r_y.at[k - 1], at(x, z, core, target)).start()

    p_t = full[...]
    gram = dot(p_t, p_t, NT, HIGHEST)
    cross = dot(p_t, pb[...], NT, HIGHEST)
    gram_all[y] = jnp.concatenate([gram, cross, jnp.zeros((R, 128 - 2 * R), F32)], axis=1)
    for k in range(1, NY):
        remote(7, gram_all.at[y], gram_all.at[y], at(x, z, core, y_peers[k - 1])).start()

    wait_on(recv.at[6], r_y)
    z_tile = s_y[y]
    for k in range(NY - 1):
        z_tile = z_tile + r_y[k]

    terms = jnp.concatenate((*three_terms(z_tile), jnp.zeros((8, 128), F32)), axis=0).astype(BF16)
    q = dot(terms, grad[lax.rem(y, 2)], NN)
    q = q[0:8] + q[8:16] + q[16:24]
    for px in range(NX):
        for k in range(NZ // 2):
            for pc in range(NC):
                t = px * NZ + 2 * k + pc
                s_q[pc, px, k] = q[:, 128 * t : 128 * (t + 1)]

    remote(8, s_q.at[other], r_qc, partner).start()
    wait_on(recv.at[8], r_qc)
    s_qx[...] = s_q[core] + r_qc[...]
    for k in range(1, NX):
        remote(9, s_qx.at[lax.rem(x + k, NX)], r_qx.at[k - 1], x_peers[k - 1]).start()
    wait_on(recv.at[9], r_qx)
    s_qz[...] = s_qx[x] + r_qx[0] + r_qx[1] + r_qx[2]

    keeps = lax.rem(z, 2) == core
    for j in range(NZ // 2):
        target = lax.rem(z + lax.rem(z + core, 2) + 2 * j, NZ)
        slot = lax.rem(z - target + NZ, NZ) - 1

        @pl.when(target != z)
        def _():
            remote(10, s_qz.at[target // 2], r_qz.at[slot], at(x, target, core, y)).start()

    wait_on(recv.at[7], gram_all.at[pl.ds(0, NY - 1)])
    sums = gram_all[0]
    for k in range(1, NY):
        sums = sums + gram_all[k]
    inverse = inverse_cholesky(sums)
    cross_all = sums[:, R : 2 * R]
    scaled = inverse * jnp.sqrt(F32(FF_ALL))
    basis_out[...] = dot(scaled, full[...], NN, HIGHEST)
    out_copy = pltpu.make_async_copy(basis_out, new_basis_t, out_sem)
    out_copy.start()
    col_tile = pl.ds(pl.multiple_of((x * NZ + z) * 128, 128), 128)
    taken = dot(cross_all, warm[:, col_tile], NN, HIGHEST)

    @pl.when(keeps)
    def _():
        wait_on(recv.at[10], r_qz)
        total = s_qz[z // 2]
        for k in range(NZ - 1):
            total = total + r_qz[k]
        s_f[...] = total
        r_f[y] = total
        remote(11, s_f, r_f.at[y], partner).start()
        for k in range(1, NY):
            for pc in (core, other):
                remote(11, s_f, r_f.at[y], at(x, z, pc, y_peers[k - 1])).start()
        wait_on(recv.at[11], r_f.at[pl.ds(0, NY - 1)])

    @pl.when(jnp.logical_not(keeps))
    def _():
        wait_on(recv.at[11], r_f)

    q_t = jnp.concatenate([r_f[2 * g] + r_f[2 * g + 1] for g in range(4)], axis=0)
    result = dot(inverse, q_t * (1.0 / REPLICAS) - taken, NN, HIGHEST)
    new_factor_t[...] = jnp.where(core == 0, result[:, 0:64], result[:, 64:128])

    wait_on(send.at[0], s_core)
    wait_on(send.at[1], r_x)

    @pl.when(owner)
    def _():
        wait_on(send.at[2], s_z.at[pl.ds(0, TILES - 1)])
        wait_on(send.at[3], r_z)

    @pl.when(jnp.logical_not(owner))
    def _():
        wait_on(send.at[2], s_z)

    wait_on(send.at[4], r_x)
    wait_on(send.at[5], r_core)
    wait_on(send.at[6], r_y)
    wait_on(send.at[7], gram_all.at[pl.ds(0, NY - 1)])
    wait_on(send.at[8], r_qc)
    wait_on(send.at[9], r_qx)

    @pl.when(keeps)
    def _():
        wait_on(send.at[10], s_qz.at[pl.ds(0, NZ // 2 - 1)])
        wait_on(send.at[11], r_qz)

    @pl.when(jnp.logical_not(keeps))
    def _():
        wait_on(send.at[10], s_qz)

    out_copy.wait()


def on_device(hidden, out_grad, prev_hidden, prev_grad, prev_basis, warm_start):
    hbm = pl.BlockSpec(memory_space=pl.ANY)
    vmem = pltpu.VMEM
    dma = pltpu.SemaphoreType.DMA
    new_basis_t, new_factor_t = pl.pallas_call(
        kernel,
        out_shape=(
            jax.ShapeDtypeStruct((R, FF), F32),
            jax.ShapeDtypeStruct((R, D // REPLICAS), F32),
        ),
        in_specs=[hbm] * 6,
        out_specs=(hbm, pl.BlockSpec(memory_space=pltpu.VMEM)),
        scratch_shapes=[
            vmem((2 * TOK, FF), BF16),
            vmem((2, TOK, D), BF16),
            vmem((R, FF), F32),
            vmem((R, D), F32),
            vmem((R, D), BF16),
            vmem((R, HALF), F32),
            vmem((R, HALF), F32),
            vmem((R, HALF), F32),
            vmem((R, HALF), F32),
            vmem((NX - 1, 8, HALF), F32),
            vmem((TILES, 8, 128), F32),
            vmem((NZ - 1, 8, 128), F32),
            vmem((R, 128), F32),
            vmem((R, FF), F32),
            vmem((8, 128), F32),
            vmem((NY, 8, 128), F32),
            vmem((NY - 1, 8, 128), F32),
            vmem((NY, R, 128), F32),
            vmem((NC, NX, NZ // 2, 8, 128), F32),
            vmem((NX, NZ // 2, 8, 128), F32),
            vmem((NX, NZ // 2, 8, 128), F32),
            vmem((NX - 1, NZ // 2, 8, 128), F32),
            vmem((NZ // 2, 8, 128), F32),
            vmem((NZ - 1, 8, 128), F32),
            vmem((8, 128), F32),
            vmem((NY, 8, 128), F32),
            vmem((R, FF), F32),
            dma((4 + 2 * G_CHUNKS,)),
            dma,
            dma((12,)),
            dma((12,)),
        ],
        compiler_params=pltpu.CompilerParams(collective_id=0, has_side_effects=True),
        name="powersgd",
    )(hidden, out_grad, prev_hidden, prev_grad, prev_basis.T, warm_start.T)
    return new_basis_t.T, new_factor_t.T


def solution(mesh):
    return jax.shard_map(
        on_device,
        mesh=mesh,
        in_specs=(
            P("dp", "tensor"),
            P("dp", None),
            P("dp", "tensor"),
            P("dp", None),
            P("tensor", None),
            P(),
        ),
        out_specs=(P("tensor", None), P("dp", None)),
        check_vma=False,
    )
```

```python
import jax
import jax.numpy as jnp
from jax import lax
from jax.experimental import pallas as pl
from jax.experimental.pallas import tpu as pltpu
from jax.sharding import PartitionSpec as P

MESH = pl.DeviceIdType.MESH
F32, BF16 = jnp.float32, jnp.bfloat16
HIGHEST = lax.Precision.HIGHEST
NT = (((1,), (1,)), ((), ()))
NN = (((1,), (0,)), ((), ()))

NX, NY, NZ, NC = 4, 8, 16, 2
R = 32
FF_ALL, FF, D, TOK = 28672, 3584, 8192, 128
REPLICAS = NX * NZ * NC
HALF = FF // NC
TILES = HALF // 128
G_CHUNKS = 4


def dot(a, b, dims, precision=None):
    return lax.dot_general(a, b, dims, precision=precision, preferred_element_type=F32)


def three_terms(v):
    a = v.astype(BF16).astype(F32)
    r = v - a
    b = r.astype(BF16).astype(F32)
    return a, b, r - b


def inverse_cholesky(gram):
    rows = lax.broadcasted_iota(jnp.int32, (R, 128), 0)
    lanes = lax.broadcasted_iota(jnp.int32, (R, 128), 1)
    m = jnp.where(lanes < R, gram, jnp.where(lanes - R == rows, 1.0, 0.0))
    for k in range(R):
        pivot = m[k : k + 1, k : k + 1]
        inv = lax.rsqrt(pivot)
        inv = inv * (1.5 - 0.5 * pivot * inv * inv)
        row = m[k : k + 1, :] * inv
        column = m[:, k : k + 1] * inv
        m = jnp.where(rows > k, m - column * row, jnp.where(rows == k, row, m))
    return m[:, R : 2 * R]


Z_FAR = (8, 7, 9, 6, 10, 5, 11, 4, 12, 3, 13, 2, 14, 1, 15)
Z_EVEN = (8, 10, 6, 12, 4, 14, 2, 16)
Y_FAR = (4, 3, 5, 2, 6, 1, 7)
X_FAR = (2, 1, 3)


def kernel(
    hidden, out_grad, prev_hidden, prev_grad, basis_t, warm_t,
    new_basis_t, new_factor_t,
    hid, grad, pb, pb_low, warm, warm_low,
    s_core, own, r_core, s_x, r_x0, r_x1, s_z, r_z, corr, full, low,
    s_y, r_y, gram_all, s_q, o_q, r_qc, s_qx, r_qx, s_qz, r_qz, s_f, r_f,
    load_sem, send, recv, owner_sem,
):
    dp, y = lax.axis_index("dp"), lax.axis_index("tensor")
    core = lax.rem(dp, NC)
    z = lax.rem(dp // NC, NZ)
    x = dp // (NC * NZ)
    other = 1 - core
    odd = lax.rem(z, 2)
    owner = jnp.logical_and(odd == 0, z < TILES)
    keeps = odd == core

    def at(px, pz, pc, py):
        return ((px * NZ + pz) * NC + pc, py)

    partner = at(x, z, other, y)
    x_peer = {k: at(lax.rem(x + k, NX), z, core, y) for k in X_FAR}
    evens = [lax.rem(z + a - odd, NZ) for a in Z_EVEN]

    def remote(phase, src, dst, device, recv_sem=None):
        return pltpu.make_async_remote_copy(
            src_ref=src, dst_ref=dst, send_sem=send.at[phase],
            recv_sem=recv.at[phase] if recv_sem is None else recv_sem,
            device_id=device, device_id_type=MESH,
        )

    def wait_on(sem, ref):
        pltpu.make_async_copy(ref, ref, sem).wait()

    def row_group(g):
        return pl.ds(pl.multiple_of(g * 8, 8), 8)

    loads = [pltpu.make_async_copy(warm_t, warm, load_sem.at[0])]
    width = D // G_CHUNKS
    for j in range(G_CHUNKS):
        cols = pl.ds(j * width, width)
        for s, g in enumerate((out_grad, prev_grad)):
            loads.append(
                pltpu.make_async_copy(g.at[:, cols], grad.at[s, :, cols], load_sem.at[1 + 2 * j + s])
            )
    n = 1 + 2 * G_CHUNKS
    loads.append(pltpu.make_async_copy(hidden, hid.at[pl.ds(0, TOK), :], load_sem.at[n]))
    loads.append(pltpu.make_async_copy(prev_hidden, hid.at[pl.ds(TOK, TOK), :], load_sem.at[n + 1]))
    loads.append(pltpu.make_async_copy(basis_t, pb, load_sem.at[n + 2]))
    for copy in loads:
        copy.start()

    barrier = pltpu.get_barrier_semaphore()

    def greet(device):
        pl.semaphore_signal(barrier, inc=1, device_id=device, device_id_type=MESH)

    greet(partner)
    for k in X_FAR:
        greet(x_peer[k])

    @pl.when(owner)
    def _():
        for k in Z_FAR:
            greet(at(x, lax.rem(z + k, NZ), core, y))

    for k in Y_FAR:
        greet(at(x, z, core, lax.rem(y + k, NY)))
        greet(at(x, z, other, lax.rem(y + k, NY)))

    loads[0].wait()
    warm_low[...] = warm[...].astype(BF16)
    acc = [jnp.zeros((R, TOK), F32), jnp.zeros((R, TOK), F32)]
    for j in range(G_CHUNKS):
        cols = slice(j * width, (j + 1) * width)
        for s in range(2):
            loads[1 + 2 * j + s].wait()
            acc[s] = acc[s] + dot(warm_low[:, cols], grad[s, :, cols], NT)
    projected = jnp.concatenate(acc, axis=1).astype(BF16)

    loads[n].wait()
    loads[n + 1].wait()
    my_half = pl.ds(pl.multiple_of(core * HALF, 128), HALF)
    chunks = ((0, 1024), (1024, HALF - 1024))
    for i, (start, size) in enumerate(chunks):
        there = pl.ds(pl.multiple_of(other * HALF + start, 128), size)
        here = pl.ds(start, size)
        s_core[:, here] = dot(projected, hid[:, there], NN)
        if i == 0:
            pl.semaphore_wait(barrier, 1 + (NX - 1) + 2 * (NY - 1) + TILES // 2 - owner.astype(jnp.int32))
        remote(i, s_core.at[:, here], r_core.at[:, here], partner).start()
    r_x = (r_x0, r_x1)
    for i, (start, size) in enumerate(chunks):
        mine = pl.ds(pl.multiple_of(core * HALF + start, 128), size)
        here = pl.ds(start, size)
        own[:, here] = dot(projected, hid[:, mine], NN)
        wait_on(recv.at[i], r_core.at[:, here])
        s_x[:, here] = own[:, here] + r_core[:, here]
        for k in X_FAR:
            remote(2 + i, s_x.at[row_group(lax.rem(x + k, NX)), here], r_x[i].at[k - 1], x_peer[k]).start()

    my_rows = row_group(x)
    for i, (start, size) in enumerate(chunks):
        wait_on(recv.at[2 + i], r_x[i])
        summed = s_x[my_rows, start : start + size] + r_x[i][0] + r_x[i][1] + r_x[i][2]
        for j in range(size // 256):
            s_z[start // 256 + j] = summed[:, 256 * j : 256 * (j + 1)]
        last = (start + size) // 128
        for target in evens:
            @pl.when(jnp.logical_and(target != z, jnp.logical_and(target >= start // 128, target < last)))
            def _():
                slot = lax.rem(z - target + NZ, NZ) - 1
                remote(4, s_z.at[target // 2], r_z.at[slot], at(x, target, core, y)).start()

    loads[n + 2].wait()
    pair = pl.ds(pl.multiple_of(core * HALF + jnp.minimum(z, TILES - 2) // 2 * 256, 256), 256)

    @pl.when(owner)
    def _():
        coupling = dot(warm[...], warm[...], NT, HIGHEST)
        corr[...] = dot(coupling, pb[:, pair], NN, HIGHEST)
        wait_on(recv.at[4], r_z)
        total = s_z[z // 2]
        for k in range(NZ - 1):
            total = total + r_z[k]
        full[my_rows, pair] = total * (1.0 / REPLICAS) - corr[my_rows, :]
        tiles = full.at[my_rows, pair]
        for k in Z_FAR:
            remote(5, tiles, tiles, at(x, lax.rem(z + k, NZ), core, y), owner_sem.at[z // 2]).start()
        for k in X_FAR:
            remote(6, tiles, tiles, x_peer[k], recv.at[5 + k]).start()

    pb_low[...] = jnp.concatenate(three_terms(pb[...]), axis=0).astype(BF16)

    for target in reversed(evens):
        @pl.when(jnp.logical_and(target != z, target < TILES))
        def _():
            tiles = full.at[my_rows, pl.ds(pl.multiple_of(core * HALF + target // 2 * 256, 256), 256)]
            wait_on(owner_sem.at[target // 2], tiles)
            for k in X_FAR:
                remote(6, tiles, tiles, x_peer[k], recv.at[5 + k]).start()

    piece = full.at[my_rows, my_half]
    remote(7, piece, piece, partner, recv.at[9]).start()
    for k in (1, 3, 2):
        piece = full.at[row_group(lax.rem(x - k + NX, NX)), my_half]
        wait_on(recv.at[5 + k], piece)
        remote(7, piece, piece, partner, recv.at[9]).start()

    def pulled_half(cols):
        low[:, cols] = jnp.concatenate(three_terms(full[:, cols]), axis=0).astype(BF16)
        return dot(low[:, cols], hid[:, cols], NT)

    zt = pulled_half(my_half)
    wait_on(recv.at[9], r_core)
    zt = zt + pulled_half(pl.ds(pl.multiple_of(other * HALF, 128), HALF))
    zt = zt[0:R] + zt[R : 2 * R] + zt[2 * R : 3 * R]

    for g in range(4):
        for s in range(2):
            s_y[2 * g + s] = zt[8 * g : 8 * (g + 1), 128 * s : 128 * (s + 1)]
    y_peer = {k: lax.rem(y + k, NY) for k in Y_FAR}
    for k in Y_FAR:
        remote(8, s_y.at[y_peer[k]], r_y.at[k - 1], at(x, z, core, y_peer[k]), recv.at[10]).start()

    def folded(m):
        m = m[0:R] + m[R : 2 * R] + m[2 * R : 3 * R]
        return m[:, 0:R] + m[:, R : 2 * R] + m[:, 2 * R : 3 * R]

    gram = folded(dot(low[...], low[...], NT))
    cross = folded(dot(low[...], pb_low[...], NT))
    gram_all[y] = jnp.concatenate([gram, cross, jnp.zeros((R, 128 - 2 * R), F32)], axis=1)
    for k in Y_FAR:
        remote(9, gram_all.at[y], gram_all.at[y], at(x, z, core, y_peer[k]), recv.at[11]).start()

    wait_on(recv.at[10], r_y)
    z_tile = s_y[y]
    for k in range(NY - 1):
        z_tile = z_tile + r_y[k]

    terms = jnp.concatenate((*three_terms(z_tile), jnp.zeros((8, 128), F32)), axis=0).astype(BF16)
    tokens = lax.rem(y, 2)
    block = NZ * 128

    def right_block(k):
        cols = pl.ds(pl.multiple_of(lax.rem(x + k, NX) * block, block), block)
        q = dot(terms, grad[tokens, :, cols], NN)
        q = q[0:8] + q[8:16] + q[16:24]
        for j in range(NZ // 2):
            even = q[:, 256 * j : 256 * j + 128]
            uneven = q[:, 256 * j + 128 : 256 * (j + 1)]
            s_q[k, j] = jnp.where(core == 0, uneven, even)
            o_q[k, j] = jnp.where(core == 0, even, uneven)
        remote(12 + k, s_q.at[k], r_qc.at[k], partner).start()

    def pass_on(k):
        wait_on(recv.at[12 + k], r_qc.at[k])
        s_qx[k] = o_q[k] + r_qc[k]
        if k:
            remote(10, s_qx.at[k], r_qx.at[k - 1], x_peer[k], recv.at[16]).start()

    right_block(2)
    right_block(1)
    right_block(3)
    pass_on(2)
    right_block(0)
    pass_on(1)
    pass_on(3)
    pass_on(0)
    wait_on(recv.at[16], r_qx)
    s_qz[...] = s_qx[0] + r_qx[0] + r_qx[1] + r_qx[2]

    for a in Z_EVEN:
        target = lax.rem(z + a - lax.rem(z + core, 2), NZ)
        slot = lax.rem(z - target + NZ, NZ) - 1

        @pl.when(target != z)
        def _():
            remote(11, s_qz.at[target // 2], r_qz.at[slot], at(x, target, core, y), recv.at[17]).start()

    wait_on(recv.at[11], gram_all.at[pl.ds(0, NY - 1)])
    sums = gram_all[0]
    for k in range(1, NY):
        sums = sums + gram_all[k]
    inverse = inverse_cholesky(sums)
    cross_all = sums[:, R : 2 * R]
    scaled = inverse * jnp.sqrt(F32(FF_ALL))
    new_basis_t[...] = dot(scaled, full[...], NN, HIGHEST)
    col_tile = pl.ds(pl.multiple_of((x * NZ + z) * 128, 128), 128)
    taken = dot(cross_all, warm[:, col_tile], NN, HIGHEST)

    @pl.when(keeps)
    def _():
        wait_on(recv.at[17], r_qz)
        total = s_qz[z // 2]
        for k in range(NZ - 1):
            total = total + r_qz[k]
        s_f[...] = total
        r_f[y] = total
        for k in Y_FAR:
            for pc in (core, other):
                remote(16, s_f, r_f.at[y], at(x, z, pc, y_peer[k]), recv.at[18]).start()
        remote(16, s_f, r_f.at[y], partner, recv.at[18]).start()
        wait_on(recv.at[18], r_f.at[pl.ds(0, NY - 1)])

    @pl.when(jnp.logical_not(keeps))
    def _():
        wait_on(recv.at[18], r_f)

    q_t = jnp.concatenate([r_f[2 * g] + r_f[2 * g + 1] for g in range(4)], axis=0)
    result = dot(inverse, q_t * (1.0 / REPLICAS) - taken, NN, HIGHEST)
    new_factor_t[...] = jnp.where(core == 0, result[:, 0:64], result[:, 64:128])

    for i, (start, size) in enumerate(chunks):
        wait_on(send.at[i], s_core.at[:, pl.ds(start, size)])
        wait_on(send.at[2 + i], r_x[i])

    @pl.when(owner)
    def _():
        wait_on(send.at[4], s_z.at[pl.ds(0, TILES // 2 - 1)])
        wait_on(send.at[5], r_z)

    @pl.when(jnp.logical_not(owner))
    def _():
        wait_on(send.at[4], s_z)

    wait_on(send.at[6], own.at[pl.ds(0, 24), :])
    wait_on(send.at[7], r_core)
    wait_on(send.at[8], r_y)
    wait_on(send.at[9], gram_all.at[pl.ds(0, NY - 1)])
    wait_on(send.at[10], r_qx)
    for k in range(NX):
        wait_on(send.at[12 + k], r_qc.at[k])

    @pl.when(keeps)
    def _():
        wait_on(send.at[11], s_qz.at[pl.ds(0, NZ // 2 - 1)])
        wait_on(send.at[16], r_qz)

    @pl.when(jnp.logical_not(keeps))
    def _():
        wait_on(send.at[11], s_qz)


def hand_over(basis, factor, new_basis_t, new_factor_t, sem):
    copies = (
        pltpu.make_async_copy(basis, new_basis_t, sem.at[0]),
        pltpu.make_async_copy(factor, new_factor_t, sem.at[1]),
    )
    for copy in copies:
        copy.start()
    for copy in copies:
        copy.wait()


def on_device(hidden, out_grad, prev_hidden, prev_grad, prev_basis, warm_start):
    hbm = pl.BlockSpec(memory_space=pl.ANY)
    vmem = pltpu.VMEM
    dma = pltpu.SemaphoreType.DMA
    results = pl.pallas_call(
        kernel,
        out_shape=(vmem((R, FF), F32), vmem((R, D // REPLICAS), F32)),
        in_specs=[hbm] * 6,
        out_specs=(pl.BlockSpec(memory_space=pltpu.VMEM),) * 2,
        scratch_shapes=[
            vmem((2 * TOK, FF), BF16),
            vmem((2, TOK, D), BF16),
            vmem((R, FF), F32),
            vmem((3 * R, FF), BF16),
            vmem((R, D), F32),
            vmem((R, D), BF16),
            vmem((R, HALF), F32),
            vmem((R, HALF), F32),
            vmem((R, HALF), F32),
            vmem((R, HALF), F32),
            vmem((NX - 1, 8, 1024), F32),
            vmem((NX - 1, 8, HALF - 1024), F32),
            vmem((TILES // 2, 8, 256), F32),
            vmem((NZ - 1, 8, 256), F32),
            vmem((R, 256), F32),
            vmem((R, FF), F32),
            vmem((3 * R, FF), BF16),
            vmem((NY, 8, 128), F32),
            vmem((NY - 1, 8, 128), F32),
            vmem((NY, R, 128), F32),
            vmem((NX, NZ // 2, 8, 128), F32),
            vmem((NX, NZ // 2, 8, 128), F32),
            vmem((NX, NZ // 2, 8, 128), F32),
            vmem((NX, NZ // 2, 8, 128), F32),
            vmem((NX - 1, NZ // 2, 8, 128), F32),
            vmem((NZ // 2, 8, 128), F32),
            vmem((NZ - 1, 8, 128), F32),
            vmem((8, 128), F32),
            vmem((NY, 8, 128), F32),
            dma((4 + 2 * G_CHUNKS,)),
            dma((17,)),
            dma((19,)),
            dma((TILES // 2,)),
        ],
        compiler_params=pltpu.CompilerParams(collective_id=0, has_side_effects=True),
        name="powersgd",
    )(hidden, out_grad, prev_hidden, prev_grad, prev_basis.T, warm_start.T)
    new_basis_t, new_factor_t = pl.pallas_call(
        hand_over,
        out_shape=(jax.ShapeDtypeStruct((R, FF), F32), jax.ShapeDtypeStruct((R, D // REPLICAS), F32)),
        in_specs=[pl.BlockSpec(memory_space=pltpu.VMEM)] * 2,
        out_specs=(hbm, hbm),
        scratch_shapes=[dma((2,))],
        name="hand_over",
    )(*(pltpu.with_memory_space_constraint(r, pltpu.VMEM) for r in results))
    return new_basis_t.T, new_factor_t.T


def solution(mesh):
    return jax.shard_map(
        on_device,
        mesh=mesh,
        in_specs=(
            P("dp", "tensor"),
            P("dp", None),
            P("dp", "tensor"),
            P("dp", None),
            P("tensor", None),
            P(),
        ),
        out_specs=(P("tensor", None), P("dp", None)),
        check_vma=False,
    )
```

```python
import jax
import jax.numpy as jnp
from jax import lax
from jax.experimental import pallas as pl
from jax.experimental.pallas import tpu as pltpu
from jax.sharding import PartitionSpec as P

MESH = pl.DeviceIdType.MESH
F32, BF16 = jnp.float32, jnp.bfloat16
HIGHEST = lax.Precision.HIGHEST
NT = (((1,), (1,)), ((), ()))
NN = (((1,), (0,)), ((), ()))

NX, NY, NZ, NC = 4, 8, 16, 2
R = 32
FF_ALL, FF, D, TOK = 28672, 3584, 8192, 128
REPLICAS = NX * NZ * NC
HALF = FF // NC
TILES = HALF // 128
G_CHUNKS = 4


def dot(a, b, dims, precision=None):
    return lax.dot_general(a, b, dims, precision=precision, preferred_element_type=F32)


def three_terms(v):
    a = v.astype(BF16).astype(F32)
    r = v - a
    b = r.astype(BF16).astype(F32)
    return a, b, r - b


def inverse_cholesky(gram):
    rows = lax.broadcasted_iota(jnp.int32, (R, 128), 0)
    lanes = lax.broadcasted_iota(jnp.int32, (R, 128), 1)
    m = jnp.where(lanes < R, gram, jnp.where(lanes - R == rows, 1.0, 0.0))
    for k in range(R):
        pivot = m[k : k + 1, k : k + 1]
        inv = lax.rsqrt(pivot)
        inv = inv * (1.5 - 0.5 * pivot * inv * inv)
        row = m[k : k + 1, :] * inv
        column = m[:, k : k + 1] * inv
        m = jnp.where(rows > k, m - column * row, jnp.where(rows == k, row, m))
    return m[:, R : 2 * R]


Z_FAR = (8, 7, 9, 6, 10, 5, 11, 4, 12, 3, 13, 2, 14, 1, 15)
Z_PAIR = (8, 10, 6, 12, 4, 14, 2, 16)
Y_FAR = (4, 3, 5, 2, 6, 1, 7)
X_FAR = (2, 1, 3)


def kernel(
    hidden, out_grad, prev_hidden, prev_grad, basis_t, warm_t,
    new_basis_t, new_factor_t,
    hid, grad, pb, pb_low, warm, warm_low,
    s_core, own, r_core, s_x, r_x0, r_x1, s_z, r_z, corr, full, low,
    s_y, r_y, gram_all, s_q, o_q, r_qc, s_qx, r_qx, s_qz, r_qz, s_f, r_f,
    load_sem, send, recv, owner_sem,
):
    dp, y = lax.axis_index("dp"), lax.axis_index("tensor")
    core = lax.rem(dp, NC)
    z = lax.rem(dp // NC, NZ)
    x = dp // (NC * NZ)
    other = 1 - core
    odd = lax.rem(z, 2)
    keeps = odd == core

    def at(px, pz, pc, py):
        return ((px * NZ + pz) * NC + pc, py)

    def owns(pz):
        return lax.rem(pz, NZ // 2) != NZ // 2 - 1

    def tile_of(pz):
        return pz - pz // (NZ // 2)

    owner = owns(z)
    partner = at(x, z, other, y)
    x_peer = {k: at(lax.rem(x + k, NX), z, core, y) for k in X_FAR}
    z_peer = {k: lax.rem(z + k, NZ) for k in Z_FAR}

    def remote(phase, src, dst, device, recv_sem=None):
        return pltpu.make_async_remote_copy(
            src_ref=src, dst_ref=dst, send_sem=send.at[phase],
            recv_sem=recv.at[phase] if recv_sem is None else recv_sem,
            device_id=device, device_id_type=MESH,
        )

    def wait_on(sem, ref):
        pltpu.make_async_copy(ref, ref, sem).wait()

    def row_group(g):
        return pl.ds(pl.multiple_of(g * 8, 8), 8)

    loads = [pltpu.make_async_copy(warm_t, warm, load_sem.at[0])]
    width = D // G_CHUNKS
    for j in range(G_CHUNKS):
        cols = pl.ds(j * width, width)
        for s, g in enumerate((out_grad, prev_grad)):
            loads.append(
                pltpu.make_async_copy(g.at[:, cols], grad.at[s, :, cols], load_sem.at[1 + 2 * j + s])
            )
    n = 1 + 2 * G_CHUNKS
    loads.append(pltpu.make_async_copy(hidden, hid.at[pl.ds(0, TOK), :], load_sem.at[n]))
    loads.append(pltpu.make_async_copy(prev_hidden, hid.at[pl.ds(TOK, TOK), :], load_sem.at[n + 1]))
    loads.append(pltpu.make_async_copy(basis_t, pb, load_sem.at[n + 2]))
    for copy in loads:
        copy.start()

    barrier = pltpu.get_barrier_semaphore()

    def greet(device):
        pl.semaphore_signal(barrier, inc=1, device_id=device, device_id_type=MESH)

    greet(partner)
    for k in X_FAR:
        greet(x_peer[k])

    @pl.when(owner)
    def _():
        for k in Z_FAR:
            greet(at(x, z_peer[k], core, y))

    for k in Y_FAR:
        greet(at(x, z, core, lax.rem(y + k, NY)))
        greet(at(x, z, other, lax.rem(y + k, NY)))

    loads[0].wait()
    warm_low[...] = warm[...].astype(BF16)
    acc = [jnp.zeros((TOK, R), F32), jnp.zeros((TOK, R), F32)]
    for j in range(G_CHUNKS):
        cols = slice(j * width, (j + 1) * width)
        for s in range(2):
            loads[1 + 2 * j + s].wait()
            acc[s] = acc[s] + dot(grad[s, :, cols], warm_low[:, cols], NT)
    projected = jnp.concatenate([a.T for a in acc], axis=1).astype(BF16)

    loads[n].wait()
    loads[n + 1].wait()
    my_half = pl.ds(pl.multiple_of(core * HALF, 128), HALF)
    chunks = ((0, 1024), (1024, HALF - 1024))
    for i, (start, size) in enumerate(chunks):
        there = pl.ds(pl.multiple_of(other * HALF + start, 128), size)
        here = pl.ds(start, size)
        s_core[:, here] = dot(projected, hid[:, there], NN)
        if i == 0:
            pl.semaphore_wait(barrier, 1 + (NX - 1) + 2 * (NY - 1) + TILES - owner.astype(jnp.int32))
        remote(i, s_core.at[:, here], r_core.at[:, here], partner).start()
    r_x = (r_x0, r_x1)
    for i, (start, size) in enumerate(chunks):
        mine = pl.ds(pl.multiple_of(core * HALF + start, 128), size)
        here = pl.ds(start, size)
        own[:, here] = dot(projected, hid[:, mine], NN)
        wait_on(recv.at[i], r_core.at[:, here])
        s_x[:, here] = own[:, here] + r_core[:, here]
        for k in X_FAR:
            remote(2 + i, s_x.at[row_group(lax.rem(x + k, NX)), here], r_x[i].at[k - 1], x_peer[k]).start()

    my_rows = row_group(x)
    for i, (start, size) in enumerate(chunks):
        wait_on(recv.at[2 + i], r_x[i])
        summed = s_x[my_rows, start : start + size] + r_x[i][0] + r_x[i][1] + r_x[i][2]
        for j in range(size // 128):
            s_z[start // 128 + j] = summed[:, 128 * j : 128 * (j + 1)]
        for k in Z_FAR:
            tile = tile_of(z_peer[k])
            in_chunk = jnp.logical_and(tile >= start // 128, tile < (start + size) // 128)

            @pl.when(jnp.logical_and(owns(z_peer[k]), in_chunk))
            def _():
                remote(4, s_z.at[tile], r_z.at[NZ - 1 - k], at(x, z_peer[k], core, y)).start()

    loads[n + 2].wait()
    my_tile = jnp.minimum(tile_of(z), TILES - 1)

    def tile_columns(tile):
        return pl.ds(pl.multiple_of(core * HALF + tile * 128, 128), 128)

    @pl.when(owner)
    def _():
        coupling = dot(warm[...], warm[...], NT, HIGHEST)
        corr[...] = dot(coupling, pb[:, tile_columns(my_tile)], NN, HIGHEST)
        wait_on(recv.at[4], r_z)
        total = s_z[my_tile]
        for k in range(NZ - 1):
            total = total + r_z[k]
        full[my_rows, tile_columns(my_tile)] = total * (1.0 / REPLICAS) - corr[my_rows, :]
        done = full.at[my_rows, tile_columns(my_tile)]
        for k in X_FAR:
            remote(6, done, done, x_peer[k], recv.at[5 + k]).start()
        for k in Z_FAR:
            remote(5, done, done, at(x, z_peer[k], core, y), owner_sem.at[my_tile]).start()

    pb_low[...] = jnp.concatenate(three_terms(pb[...]), axis=0).astype(BF16)

    for k in reversed(Z_FAR):
        tile = tile_of(z_peer[k])

        @pl.when(owns(z_peer[k]))
        def _():
            done = full.at[my_rows, tile_columns(tile)]
            wait_on(owner_sem.at[tile], done)
            for i in X_FAR:
                remote(6, done, done, x_peer[i], recv.at[5 + i]).start()

    piece = full.at[my_rows, my_half]
    remote(7, piece, piece, partner, recv.at[9]).start()
    for k in (1, 3, 2):
        piece = full.at[row_group(lax.rem(x - k + NX, NX)), my_half]
        wait_on(recv.at[5 + k], piece)
        remote(7, piece, piece, partner, recv.at[9]).start()

    def pulled_half(cols):
        low[:, cols] = jnp.concatenate(three_terms(full[:, cols]), axis=0).astype(BF16)
        return dot(low[:, cols], hid[:, cols], NT)

    zt = pulled_half(my_half)
    wait_on(recv.at[9], r_core)
    zt = zt + pulled_half(pl.ds(pl.multiple_of(other * HALF, 128), HALF))
    zt = zt[0:R] + zt[R : 2 * R] + zt[2 * R : 3 * R]

    for g in range(4):
        for s in range(2):
            s_y[2 * g + s] = zt[8 * g : 8 * (g + 1), 128 * s : 128 * (s + 1)]
    y_peer = {k: lax.rem(y + k, NY) for k in Y_FAR}
    for k in Y_FAR:
        remote(8, s_y.at[y_peer[k]], r_y.at[k - 1], at(x, z, core, y_peer[k]), recv.at[10]).start()

    def folded(m):
        m = m[0:R] + m[R : 2 * R] + m[2 * R : 3 * R]
        return m[:, 0:R] + m[:, R : 2 * R] + m[:, 2 * R : 3 * R]

    gram = folded(dot(low[...], low[...], NT))
    cross = folded(dot(low[...], pb_low[...], NT))
    gram_all[y] = jnp.concatenate([gram, cross, jnp.zeros((R, 128 - 2 * R), F32)], axis=1)
    wait_on(recv.at[10], r_y)
    z_tile = s_y[y]
    for k in range(NY - 1):
        z_tile = z_tile + r_y[k]
    for k in Y_FAR:
        remote(9, gram_all.at[y], gram_all.at[y], at(x, z, core, y_peer[k]), recv.at[11]).start()

    terms = jnp.concatenate((*three_terms(z_tile), jnp.zeros((8, 128), F32)), axis=0).astype(BF16)
    tokens = lax.rem(y, 2)
    block = NZ * 128

    def right_block(k):
        cols = pl.ds(pl.multiple_of(lax.rem(x + k, NX) * block, block), block)
        q = dot(terms, grad[tokens, :, cols], NN)
        q = q[0:8] + q[8:16] + q[16:24]
        for j in range(NZ // 2):
            even = q[:, 256 * j : 256 * j + 128]
            uneven = q[:, 256 * j + 128 : 256 * (j + 1)]
            s_q[k, j] = jnp.where(core == 0, uneven, even)
            o_q[k, j] = jnp.where(core == 0, even, uneven)
        remote(12 + k, s_q.at[k], r_qc.at[k], partner).start()

    def pass_on(k):
        wait_on(recv.at[12 + k], r_qc.at[k])
        s_qx[k] = o_q[k] + r_qc[k]
        if k:
            remote(10, s_qx.at[k], r_qx.at[k - 1], x_peer[k], recv.at[16]).start()

    right_block(2)
    right_block(1)
    right_block(3)
    pass_on(2)
    right_block(0)
    pass_on(1)
    pass_on(3)
    pass_on(0)
    wait_on(recv.at[16], r_qx)
    s_qz[...] = s_qx[0] + r_qx[0] + r_qx[1] + r_qx[2]

    for a in Z_PAIR:
        target = lax.rem(z + a - lax.rem(z + core, 2), NZ)
        slot = lax.rem(z - target + NZ, NZ) - 1

        @pl.when(target != z)
        def _():
            remote(11, s_qz.at[target // 2], r_qz.at[slot], at(x, target, core, y), recv.at[17]).start()

    wait_on(recv.at[11], gram_all.at[pl.ds(0, NY - 1)])
    sums = gram_all[0]
    for k in range(1, NY):
        sums = sums + gram_all[k]
    inverse = inverse_cholesky(sums)
    cross_all = sums[:, R : 2 * R]
    scaled = inverse * jnp.sqrt(F32(FF_ALL))
    new_basis_t[...] = dot(scaled, full[...], NN, HIGHEST)
    col_tile = pl.ds(pl.multiple_of((x * NZ + z) * 128, 128), 128)
    taken = dot(cross_all, warm[:, col_tile], NN, HIGHEST)

    @pl.when(keeps)
    def _():
        wait_on(recv.at[17], r_qz)
        total = s_qz[z // 2]
        for k in range(NZ - 1):
            total = total + r_qz[k]
        s_f[...] = total
        r_f[y] = total
        for k in Y_FAR:
            for pc in (core, other):
                remote(16, s_f, r_f.at[y], at(x, z, pc, y_peer[k]), recv.at[18]).start()
        remote(16, s_f, r_f.at[y], partner, recv.at[18]).start()
        wait_on(recv.at[18], r_f.at[pl.ds(0, NY - 1)])

    @pl.when(jnp.logical_not(keeps))
    def _():
        wait_on(recv.at[18], r_f)

    q_t = jnp.concatenate([r_f[2 * g] + r_f[2 * g + 1] for g in range(4)], axis=0)
    result = dot(inverse, q_t * (1.0 / REPLICAS) - taken, NN, HIGHEST)
    new_factor_t[...] = jnp.where(core == 0, result[:, 0:64], result[:, 64:128])

    for i, (start, size) in enumerate(chunks):
        wait_on(send.at[i], s_core.at[:, pl.ds(start, size)])
        wait_on(send.at[2 + i], r_x[i])

    @pl.when(owner)
    def _():
        wait_on(send.at[4], s_z.at[pl.ds(0, TILES - 1)])
        wait_on(send.at[5], r_z)

    @pl.when(jnp.logical_not(owner))
    def _():
        wait_on(send.at[4], s_z)

    wait_on(send.at[6], own.at[pl.ds(0, 24), :])
    wait_on(send.at[7], r_core)
    wait_on(send.at[8], r_y)
    wait_on(send.at[9], gram_all.at[pl.ds(0, NY - 1)])
    wait_on(send.at[10], r_qx)
    for k in range(NX):
        wait_on(send.at[12 + k], r_qc.at[k])

    @pl.when(keeps)
    def _():
        wait_on(send.at[11], s_qz.at[pl.ds(0, NZ // 2 - 1)])
        wait_on(send.at[16], r_qz)

    @pl.when(jnp.logical_not(keeps))
    def _():
        wait_on(send.at[11], s_qz)


def hand_over(basis, factor, new_basis_t, new_factor_t, sem):
    copies = (
        pltpu.make_async_copy(basis, new_basis_t, sem.at[0]),
        pltpu.make_async_copy(factor, new_factor_t, sem.at[1]),
    )
    for copy in copies:
        copy.start()
    for copy in copies:
        copy.wait()


def on_device(hidden, out_grad, prev_hidden, prev_grad, prev_basis, warm_start):
    hbm = pl.BlockSpec(memory_space=pl.ANY)
    vmem = pltpu.VMEM
    dma = pltpu.SemaphoreType.DMA
    results = pl.pallas_call(
        kernel,
        out_shape=(vmem((R, FF), F32), vmem((R, D // REPLICAS), F32)),
        in_specs=[hbm] * 6,
        out_specs=(pl.BlockSpec(memory_space=pltpu.VMEM),) * 2,
        scratch_shapes=[
            vmem((2 * TOK, FF), BF16),
            vmem((2, TOK, D), BF16),
            vmem((R, FF), F32),
            vmem((3 * R, FF), BF16),
            vmem((R, D), F32),
            vmem((R, D), BF16),
            vmem((R, HALF), F32),
            vmem((R, HALF), F32),
            vmem((R, HALF), F32),
            vmem((R, HALF), F32),
            vmem((NX - 1, 8, 1024), F32),
            vmem((NX - 1, 8, HALF - 1024), F32),
            vmem((TILES, 8, 128), F32),
            vmem((NZ - 1, 8, 128), F32),
            vmem((R, 128), F32),
            vmem((R, FF), F32),
            vmem((3 * R, FF), BF16),
            vmem((NY, 8, 128), F32),
            vmem((NY - 1, 8, 128), F32),
            vmem((NY, R, 128), F32),
            vmem((NX, NZ // 2, 8, 128), F32),
            vmem((NX, NZ // 2, 8, 128), F32),
            vmem((NX, NZ // 2, 8, 128), F32),
            vmem((NX, NZ // 2, 8, 128), F32),
            vmem((NX - 1, NZ // 2, 8, 128), F32),
            vmem((NZ // 2, 8, 128), F32),
            vmem((NZ - 1, 8, 128), F32),
            vmem((8, 128), F32),
            vmem((NY, 8, 128), F32),
            dma((4 + 2 * G_CHUNKS,)),
            dma((17,)),
            dma((19,)),
            dma((TILES,)),
        ],
        compiler_params=pltpu.CompilerParams(collective_id=0, has_side_effects=True),
        name="powersgd",
    )(hidden, out_grad, prev_hidden, prev_grad, prev_basis.T, warm_start.T)
    new_basis_t, new_factor_t = pl.pallas_call(
        hand_over,
        out_shape=(jax.ShapeDtypeStruct((R, FF), F32), jax.ShapeDtypeStruct((R, D // REPLICAS), F32)),
        in_specs=[pl.BlockSpec(memory_space=pltpu.VMEM)] * 2,
        out_specs=(hbm, hbm),
        scratch_shapes=[dma((2,))],
        name="hand_over",
    )(*(pltpu.with_memory_space_constraint(r, pltpu.VMEM) for r in results))
    return new_basis_t.T, new_factor_t.T


def solution(mesh):
    return jax.shard_map(
        on_device,
        mesh=mesh,
        in_specs=(
            P("dp", "tensor"),
            P("dp", None),
            P("dp", "tensor"),
            P("dp", None),
            P("tensor", None),
            P(),
        ),
        out_specs=(P("tensor", None), P("dp", None)),
        check_vma=False,
    )
```

```python
import jax
import jax.numpy as jnp
from jax import lax
from jax.experimental import pallas as pl
from jax.experimental.pallas import tpu as pltpu
from jax.sharding import PartitionSpec as P

MESH = pl.DeviceIdType.MESH
F32, BF16 = jnp.float32, jnp.bfloat16
HIGHEST = lax.Precision.HIGHEST
NT = (((1,), (1,)), ((), ()))
NN = (((1,), (0,)), ((), ()))

NX, NY, NZ, NC = 4, 8, 16, 2
R = 32
FF_ALL, FF, D, TOK = 28672, 3584, 8192, 128
REPLICAS = NX * NZ * NC
HALF = FF // NC
TILES = HALF // 128
G_CHUNKS = 4


def dot(a, b, dims, precision=None):
    return lax.dot_general(a, b, dims, precision=precision, preferred_element_type=F32)


def three_terms(v):
    a = v.astype(BF16).astype(F32)
    r = v - a
    b = r.astype(BF16).astype(F32)
    return a, b, r - b


def inverse_cholesky(gram):
    rows = lax.broadcasted_iota(jnp.int32, (R, 128), 0)
    lanes = lax.broadcasted_iota(jnp.int32, (R, 128), 1)
    m = jnp.where(lanes < R, gram, jnp.where(lanes - R == rows, 1.0, 0.0))
    for k in range(R):
        pivot = m[k : k + 1, k : k + 1]
        inv = lax.rsqrt(pivot)
        inv = inv * (1.5 - 0.5 * pivot * inv * inv)
        row = m[k : k + 1, :] * inv
        column = m[:, k : k + 1] * inv
        m = jnp.where(rows > k, m - column * row, jnp.where(rows == k, row, m))
    return m[:, R : 2 * R]


Z_FAR = (8, 7, 9, 6, 10, 5, 11, 4, 12, 3, 13, 2, 14, 1, 15)
Z_PAIR = (8, 10, 6, 12, 4, 14, 2, 16)
Y_FAR = (4, 3, 5, 2, 6, 1, 7)
X_FAR = (2, 1, 3)


def kernel(
    hidden, out_grad, prev_hidden, prev_grad, basis_t, warm_t,
    new_basis_t, new_factor_t,
    hid, grad, pb, pb_low, warm, warm_low,
    s_core, own, r_core, s_x, r_x0, r_x1, s_z, r_z, corr, full, low,
    s_y, r_y, gram_all, s_q, o_q, r_qc, s_qx, r_qx, s_qz, r_qz, s_f, r_f,
    load_sem, send, recv, owner_sem,
):
    dp, y = lax.axis_index("dp"), lax.axis_index("tensor")
    core = lax.rem(dp, NC)
    z = lax.rem(dp // NC, NZ)
    x = dp // (NC * NZ)
    other = 1 - core
    odd = lax.rem(z, 2)
    keeps = odd == core

    def at(px, pz, pc, py):
        return ((px * NZ + pz) * NC + pc, py)

    def owns(pz):
        return lax.rem(pz, NZ // 2) != NZ // 2 - 1

    def tile_of(pz):
        return pz - pz // (NZ // 2)

    owner = owns(z)
    partner = at(x, z, other, y)
    x_peer = {k: at(lax.rem(x + k, NX), z, core, y) for k in X_FAR}
    z_peer = {k: lax.rem(z + k, NZ) for k in Z_FAR}

    def remote(phase, src, dst, device, recv_sem=None):
        return pltpu.make_async_remote_copy(
            src_ref=src, dst_ref=dst, send_sem=send.at[phase],
            recv_sem=recv.at[phase] if recv_sem is None else recv_sem,
            device_id=device, device_id_type=MESH,
        )

    def wait_on(sem, ref):
        pltpu.make_async_copy(ref, ref, sem).wait()

    def row_group(g):
        return pl.ds(pl.multiple_of(g * 8, 8), 8)

    loads = [pltpu.make_async_copy(warm_t, warm, load_sem.at[0])]
    width = D // G_CHUNKS
    for j in range(G_CHUNKS):
        cols = pl.ds(j * width, width)
        for s, g in enumerate((out_grad, prev_grad)):
            loads.append(
                pltpu.make_async_copy(g.at[:, cols], grad.at[s, :, cols], load_sem.at[1 + 2 * j + s])
            )
    n = 1 + 2 * G_CHUNKS
    my_half = pl.ds(pl.multiple_of(core * HALF, 128), HALF)
    other_half = pl.ds(pl.multiple_of(other * HALF, 128), HALF)
    for i, cols in enumerate((other_half, my_half)):
        for s, h in enumerate((hidden, prev_hidden)):
            loads.append(
                pltpu.make_async_copy(h.at[:, cols], hid.at[pl.ds(s * TOK, TOK), cols], load_sem.at[n + 2 * i + s])
            )
    loads.append(pltpu.make_async_copy(basis_t, pb, load_sem.at[n + 4]))
    for copy in loads:
        copy.start()

    barrier = pltpu.get_barrier_semaphore()

    def greet(device):
        pl.semaphore_signal(barrier, inc=1, device_id=device, device_id_type=MESH)

    greet(partner)
    for k in X_FAR:
        greet(x_peer[k])

    @pl.when(owner)
    def _():
        for k in Z_FAR:
            greet(at(x, z_peer[k], core, y))

    for k in Y_FAR:
        greet(at(x, z, core, lax.rem(y + k, NY)))
        greet(at(x, z, other, lax.rem(y + k, NY)))

    loads[0].wait()
    warm_low[...] = warm[...].astype(BF16)
    acc = [jnp.zeros((TOK, R), F32), jnp.zeros((TOK, R), F32)]
    for j in range(G_CHUNKS):
        cols = slice(j * width, (j + 1) * width)
        for s in range(2):
            loads[1 + 2 * j + s].wait()
            acc[s] = acc[s] + dot(grad[s, :, cols], warm_low[:, cols], NT)
    projected = jnp.concatenate([a.T for a in acc], axis=1).astype(BF16)

    loads[n].wait()
    loads[n + 1].wait()
    chunks = ((0, 1024), (1024, HALF - 1024))
    for i, (start, size) in enumerate(chunks):
        there = pl.ds(pl.multiple_of(other * HALF + start, 128), size)
        here = pl.ds(start, size)
        s_core[:, here] = dot(projected, hid[:, there], NN)
        if i == 0:
            pl.semaphore_wait(barrier, 1 + (NX - 1) + 2 * (NY - 1) + TILES - owner.astype(jnp.int32))
        remote(i, s_core.at[:, here], r_core.at[:, here], partner).start()
    r_x = (r_x0, r_x1)
    loads[n + 2].wait()
    loads[n + 3].wait()
    for i, (start, size) in enumerate(chunks):
        mine = pl.ds(pl.multiple_of(core * HALF + start, 128), size)
        here = pl.ds(start, size)
        own[:, here] = dot(projected, hid[:, mine], NN)
        wait_on(recv.at[i], r_core.at[:, here])
        s_x[:, here] = own[:, here] + r_core[:, here]
        for k in X_FAR:
            remote(2 + i, s_x.at[row_group(lax.rem(x + k, NX)), here], r_x[i].at[k - 1], x_peer[k]).start()

    my_rows = row_group(x)
    for i, (start, size) in enumerate(chunks):
        wait_on(recv.at[2 + i], r_x[i])
        summed = s_x[my_rows, start : start + size] + r_x[i][0] + r_x[i][1] + r_x[i][2]
        for j in range(size // 128):
            s_z[start // 128 + j] = summed[:, 128 * j : 128 * (j + 1)]
        for k in Z_FAR:
            tile = tile_of(z_peer[k])
            in_chunk = jnp.logical_and(tile >= start // 128, tile < (start + size) // 128)

            @pl.when(jnp.logical_and(owns(z_peer[k]), in_chunk))
            def _():
                remote(4, s_z.at[tile], r_z.at[NZ - 1 - k], at(x, z_peer[k], core, y)).start()

    loads[n + 4].wait()
    my_tile = jnp.minimum(tile_of(z), TILES - 1)

    def tile_columns(tile):
        return pl.ds(pl.multiple_of(core * HALF + tile * 128, 128), 128)

    @pl.when(owner)
    def _():
        coupling = dot(warm[...], warm[...], NT, HIGHEST)
        corr[...] = dot(coupling, pb[:, tile_columns(my_tile)], NN, HIGHEST)
        wait_on(recv.at[4], r_z)
        total = s_z[my_tile]
        for k in range(NZ - 1):
            total = total + r_z[k]
        full[my_rows, tile_columns(my_tile)] = total * (1.0 / REPLICAS) - corr[my_rows, :]
        done = full.at[my_rows, tile_columns(my_tile)]
        for k in X_FAR:
            remote(6, done, done, x_peer[k], recv.at[5 + k]).start()
        for k in Z_FAR:
            remote(5, done, done, at(x, z_peer[k], core, y), owner_sem.at[my_tile]).start()

    pb_low[...] = jnp.concatenate(three_terms(pb[...]), axis=0).astype(BF16)

    for k in reversed(Z_FAR):
        tile = tile_of(z_peer[k])

        @pl.when(owns(z_peer[k]))
        def _():
            done = full.at[my_rows, tile_columns(tile)]
            wait_on(owner_sem.at[tile], done)
            for i in X_FAR:
                remote(6, done, done, x_peer[i], recv.at[5 + i]).start()

    piece = full.at[my_rows, my_half]
    remote(7, piece, piece, partner, recv.at[9]).start()
    for k in (1, 3, 2):
        piece = full.at[row_group(lax.rem(x - k + NX, NX)), my_half]
        wait_on(recv.at[5 + k], piece)
        remote(7, piece, piece, partner, recv.at[9]).start()

    def pulled_half(cols):
        low[:, cols] = jnp.concatenate(three_terms(full[:, cols]), axis=0).astype(BF16)
        return dot(low[:, cols], hid[:, cols], NT)

    zt = pulled_half(my_half)
    wait_on(recv.at[9], r_core)
    zt = zt + pulled_half(other_half)
    zt = zt[0:R] + zt[R : 2 * R] + zt[2 * R : 3 * R]

    for g in range(4):
        for s in range(2):
            s_y[2 * g + s] = zt[8 * g : 8 * (g + 1), 128 * s : 128 * (s + 1)]
    y_peer = {k: lax.rem(y + k, NY) for k in Y_FAR}
    for k in Y_FAR:
        remote(8, s_y.at[y_peer[k]], r_y.at[k - 1], at(x, z, core, y_peer[k]), recv.at[10]).start()

    def folded(m):
        m = m[0:R] + m[R : 2 * R] + m[2 * R : 3 * R]
        return m[:, 0:R] + m[:, R : 2 * R] + m[:, 2 * R : 3 * R]

    gram = folded(dot(low[...], low[...], NT))
    cross = folded(dot(low[...], pb_low[...], NT))
    gram_all[y] = jnp.concatenate([gram, cross, jnp.zeros((R, 128 - 2 * R), F32)], axis=1)
    wait_on(recv.at[10], r_y)
    z_tile = s_y[y]
    for k in range(NY - 1):
        z_tile = z_tile + r_y[k]
    for k in Y_FAR:
        remote(9, gram_all.at[y], gram_all.at[y], at(x, z, core, y_peer[k]), recv.at[11]).start()

    terms = jnp.concatenate((*three_terms(z_tile), jnp.zeros((8, 128), F32)), axis=0).astype(BF16)
    tokens = lax.rem(y, 2)
    block = NZ * 128

    def right_block(k):
        cols = pl.ds(pl.multiple_of(lax.rem(x + k, NX) * block, block), block)
        q = dot(terms, grad[tokens, :, cols], NN)
        q = q[0:8] + q[8:16] + q[16:24]
        for j in range(NZ // 2):
            even = q[:, 256 * j : 256 * j + 128]
            uneven = q[:, 256 * j + 128 : 256 * (j + 1)]
            s_q[k, j] = jnp.where(core == 0, uneven, even)
            o_q[k, j] = jnp.where(core == 0, even, uneven)
        remote(12 + k, s_q.at[k], r_qc.at[k], partner).start()

    def pass_on(k):
        wait_on(recv.at[12 + k], r_qc.at[k])
        s_qx[k] = o_q[k] + r_qc[k]
        if k:
            remote(10, s_qx.at[k], r_qx.at[k - 1], x_peer[k], recv.at[16]).start()

    right_block(2)
    right_block(1)
    right_block(3)
    pass_on(2)
    right_block(0)
    pass_on(1)
    pass_on(3)
    pass_on(0)
    wait_on(recv.at[16], r_qx)
    s_qz[...] = s_qx[0] + r_qx[0] + r_qx[1] + r_qx[2]

    for a in Z_PAIR:
        target = lax.rem(z + a - lax.rem(z + core, 2), NZ)
        slot = lax.rem(z - target + NZ, NZ) - 1

        @pl.when(target != z)
        def _():
            remote(11, s_qz.at[target // 2], r_qz.at[slot], at(x, target, core, y), recv.at[17]).start()

    wait_on(recv.at[11], gram_all.at[pl.ds(0, NY - 1)])
    sums = gram_all[0]
    for k in range(1, NY):
        sums = sums + gram_all[k]
    inverse = inverse_cholesky(sums)
    i1, i2, i3 = three_terms(inverse)
    inverse_terms = jnp.concatenate([i1, i1, i1, i2, i2, i3], axis=1).astype(BF16)
    cross_all = sums[:, R : 2 * R]
    scaled = inverse * jnp.sqrt(F32(FF_ALL))
    new_basis_t[...] = dot(scaled, full[...], NN, HIGHEST)
    col_tile = pl.ds(pl.multiple_of((x * NZ + z) * 128, 128), 128)
    taken = dot(cross_all, warm[:, col_tile], NN, HIGHEST)

    @pl.when(keeps)
    def _():
        wait_on(recv.at[17], r_qz)
        total = s_qz[z // 2]
        for k in range(NZ - 1):
            total = total + r_qz[k]
        s_f[...] = total
        r_f[y] = total
        for k in Y_FAR:
            for pc in (core, other):
                remote(16, s_f, r_f.at[y], at(x, z, pc, y_peer[k]), recv.at[18]).start()
        remote(16, s_f, r_f.at[y], partner, recv.at[18]).start()

    for i, (start, size) in enumerate(chunks):
        wait_on(send.at[i], s_core.at[:, pl.ds(start, size)])
        wait_on(send.at[2 + i], r_x[i])

    @pl.when(owner)
    def _():
        wait_on(send.at[4], s_z.at[pl.ds(0, TILES - 1)])
        wait_on(send.at[5], r_z)

    @pl.when(jnp.logical_not(owner))
    def _():
        wait_on(send.at[4], s_z)

    wait_on(send.at[6], own.at[pl.ds(0, 24), :])
    wait_on(send.at[7], r_core)
    wait_on(send.at[8], r_y)
    wait_on(send.at[9], gram_all.at[pl.ds(0, NY - 1)])
    wait_on(send.at[10], r_qx)
    for k in range(NX):
        wait_on(send.at[12 + k], r_qc.at[k])

    @pl.when(keeps)
    def _():
        wait_on(send.at[11], s_qz.at[pl.ds(0, NZ // 2 - 1)])

    @pl.when(jnp.logical_not(keeps))
    def _():
        wait_on(send.at[11], s_qz)

    @pl.when(keeps)
    def _():
        wait_on(recv.at[18], r_f.at[pl.ds(0, NY - 1)])

    @pl.when(jnp.logical_not(keeps))
    def _():
        wait_on(recv.at[18], r_f)

    q_t = jnp.concatenate([r_f[2 * g] + r_f[2 * g + 1] for g in range(4)], axis=0)
    q1, q2, q3 = three_terms(q_t * (1.0 / REPLICAS) - taken)
    result = dot(inverse_terms, jnp.concatenate([q1, q2, q3, q1, q2, q1], axis=0).astype(BF16), NN)
    new_factor_t[...] = jnp.where(core == 0, result[:, 0:64], result[:, 64:128])

    @pl.when(keeps)
    def _():
        wait_on(send.at[16], r_qz)


def hand_over(basis, factor, new_basis_t, new_factor_t, sem):
    copies = (
        pltpu.make_async_copy(basis, new_basis_t, sem.at[0]),
        pltpu.make_async_copy(factor, new_factor_t, sem.at[1]),
    )
    for copy in copies:
        copy.start()
    for copy in copies:
        copy.wait()


def on_device(hidden, out_grad, prev_hidden, prev_grad, prev_basis, warm_start):
    hbm = pl.BlockSpec(memory_space=pl.ANY)
    vmem = pltpu.VMEM
    dma = pltpu.SemaphoreType.DMA
    results = pl.pallas_call(
        kernel,
        out_shape=(vmem((R, FF), F32), vmem((R, D // REPLICAS), F32)),
        in_specs=[hbm] * 6,
        out_specs=(pl.BlockSpec(memory_space=pltpu.VMEM),) * 2,
        scratch_shapes=[
            vmem((2 * TOK, FF), BF16),
            vmem((2, TOK, D), BF16),
            vmem((R, FF), F32),
            vmem((3 * R, FF), BF16),
            vmem((R, D), F32),
            vmem((R, D), BF16),
            vmem((R, HALF), F32),
            vmem((R, HALF), F32),
            vmem((R, HALF), F32),
            vmem((R, HALF), F32),
            vmem((NX - 1, 8, 1024), F32),
            vmem((NX - 1, 8, HALF - 1024), F32),
            vmem((TILES, 8, 128), F32),
            vmem((NZ - 1, 8, 128), F32),
            vmem((R, 128), F32),
            vmem((R, FF), F32),
            vmem((3 * R, FF), BF16),
            vmem((NY, 8, 128), F32),
            vmem((NY - 1, 8, 128), F32),
            vmem((NY, R, 128), F32),
            vmem((NX, NZ // 2, 8, 128), F32),
            vmem((NX, NZ // 2, 8, 128), F32),
            vmem((NX, NZ // 2, 8, 128), F32),
            vmem((NX, NZ // 2, 8, 128), F32),
            vmem((NX - 1, NZ // 2, 8, 128), F32),
            vmem((NZ // 2, 8, 128), F32),
            vmem((NZ - 1, 8, 128), F32),
            vmem((8, 128), F32),
            vmem((NY, 8, 128), F32),
            dma((6 + 2 * G_CHUNKS,)),
            dma((17,)),
            dma((19,)),
            dma((TILES,)),
        ],
        compiler_params=pltpu.CompilerParams(collective_id=0, has_side_effects=True),
        name="powersgd",
    )(hidden, out_grad, prev_hidden, prev_grad, prev_basis.T, warm_start.T)
    new_basis_t, new_factor_t = pl.pallas_call(
        hand_over,
        out_shape=(jax.ShapeDtypeStruct((R, FF), F32), jax.ShapeDtypeStruct((R, D // REPLICAS), F32)),
        in_specs=[pl.BlockSpec(memory_space=pltpu.VMEM)] * 2,
        out_specs=(hbm, hbm),
        scratch_shapes=[dma((2,))],
        name="hand_over",
    )(*(pltpu.with_memory_space_constraint(r, pltpu.VMEM) for r in results))
    return new_basis_t.T, new_factor_t.T


def solution(mesh):
    return jax.shard_map(
        on_device,
        mesh=mesh,
        in_specs=(
            P("dp", "tensor"),
            P("dp", None),
            P("dp", "tensor"),
            P("dp", None),
            P("tensor", None),
            P(),
        ),
        out_specs=(P("tensor", None), P("dp", None)),
        check_vma=False,
    )
```
